32 devices in a mesh: ctx: 32 (over z, y, x, core).
Axes of the slice: x: 2, y: 2, z: 4, core: 2. Of those that a mesh axis runs over, the one named last changes fastest.
Arguments:
- queries: bfloat16 [4096, 32, 128], P('ctx'), may hold values from -40 to 40
- keys: bfloat16 [4096, 32, 128], P('ctx'), may hold values from -40 to 40
- values: bfloat16 [4096, 32, 128], P('ctx'), may hold values from -6 to 6
- cu_seqlens: int32 [17], replicated, may hold values from 0 to 4096, as said below
- positions: int32 [4096], P('ctx'), may hold values from 0 to 511, as said below
Outputs:
- attended: bfloat16 [4096, 32, 128], P('ctx')
The draws below stay inside these ranges and needn't reach their ends.
Inputs may be any that keep to these rules, and one draw needn't show every extreme that they name: `cu_seqlens`: document starts in increasing order followed by 4096; the first start is 0, every document holds at least one token, exactly one document holds 512 tokens and every other fewer. `positions`: each token's offset from the start of its document as given by cu_seqlens.
All inputs are finite; a program needn't handle non-finite values.
Results may differ from the reference program's by a relative error of at most 0.0059.
Values may be sent and summed in bfloat16 or wider, within the bound.
No kernel may reach another device: no remote copies, remote signals or barrier semaphores. Data moves between devices by JAX's collectives and lax.ppermute only.
A program may use at most 192 MiB of HBM per device.

```python
import jax
import jax.numpy as jnp
from jax import lax

HEAD_DIM = 128
HEADS = 32
DOCS = 16
TOKENS = 4096
DOC_MOST = 512


def doc_layout(key):
    base = jax.random.fold_in(key, 11)
    cut_key, place_key = jax.random.split(base, 2)
    rest = TOKENS - DOC_MOST
    others = DOCS - 1
    jitter = rest // (4 * others)
    inner = jnp.arange(1, others, dtype=jnp.int32)
    shifts = jax.random.randint(cut_key, (others - 1,), -jitter, jitter + 1).astype(jnp.int32)
    cuts = (inner * rest // others + shifts).astype(jnp.int32)
    edges = jnp.concatenate([jnp.zeros((1,), jnp.int32), cuts, jnp.full((1,), rest, jnp.int32)])
    small = (edges[1:] - edges[:-1]).astype(jnp.int32)
    slot = jax.random.randint(place_key, (), 0, DOCS)
    index = jnp.arange(DOCS, dtype=jnp.int32)
    source = jnp.clip(index - (index > slot).astype(jnp.int32), 0, DOCS - 2)
    lengths = jnp.where(index == slot, DOC_MOST, small[source]).astype(jnp.int32)
    starts = jnp.concatenate([jnp.zeros((1,), jnp.int32), jnp.cumsum(lengths).astype(jnp.int32)])
    return starts.astype(jnp.int32)


def draw_cu_seqlens(key, part):
    return doc_layout(key)


def draw_positions(key, part):
    starts = doc_layout(key)
    offsets = jnp.arange(TOKENS, dtype=jnp.int32)
    counted = jnp.sum((starts[None, :DOCS] <= offsets[:, None]).astype(jnp.int32), axis=1) - 1
    return (offsets - starts[counted]).astype(jnp.int32)


def drawn_pair(key):
    base = jax.random.fold_in(key, 23)
    query_seed, key_seed = jax.random.split(base, 2)
    array_shape = (TOKENS, HEADS, HEAD_DIM)
    query_draw = jnp.clip(jax.random.normal(query_seed, array_shape, jnp.float32), -6.0, 6.0)
    key_draw = jnp.clip(jax.random.normal(key_seed, array_shape, jnp.float32), -6.0, 6.0)
    return (query_draw, key_draw)


def draw_queries(key, part):
    return drawn_pair(key)[0].astype(jnp.bfloat16)


def draw_keys(key, part):
    return drawn_pair(key)[1].astype(jnp.bfloat16)


def block_scale(key, dims, cuts, low, top_value):
    level, own = 1.0, jax.random.fold_in(key, 6)
    for axis_at, shards_of in cuts:
        draws = jnp.exp(jax.random.uniform(jax.random.fold_in(own, axis_at), (shards_of,), jnp.float32, low / len(cuts), top_value / len(cuts)))
        level = level * jnp.repeat(draws, dims[axis_at] // shards_of).reshape([-1 if axis == axis_at else 1 for axis in range(len(dims))])
    return level


def scatter_about(stream_key, extent, deviation, bound, cuts=(), held_as=jnp.bfloat16):
    entries = jax.random.normal(stream_key, extent, jnp.float32) * deviation
    if len(cuts) > 0:
        entries = block_scale(stream_key, extent, cuts, -0.22, 0.18) * entries
    return jnp.clip(entries, min=-bound, max=bound).astype(held_as)


def setup_inputs(seed: int = 0) -> dict:
    seeds = jax.random.split(jax.random.key(seed), 6)
    queries = draw_queries(jax.random.fold_in(seeds[5], 71), 0)
    keys = draw_keys(jax.random.fold_in(seeds[5], 71), 0)
    values = scatter_about(seeds[2], (TOKENS, HEADS, HEAD_DIM), 1.0, 6.0, ((0, 32),))
    cu_seqlens = draw_cu_seqlens(jax.random.fold_in(seeds[5], 71), 0)
    positions = draw_positions(jax.random.fold_in(seeds[5], 71), 0)
    return dict(queries=queries, keys=keys, values=values, cu_seqlens=cu_seqlens, positions=positions)


rope_base = 500000.0
query_blocks = 16


def rotate(inputs, places):
    half_width = inputs.shape[-1] // 2
    ladder = jnp.arange(half_width, dtype=jnp.float32) * (2.0 / inputs.shape[-1])
    frequency = jnp.power(jnp.float32(rope_base), -ladder)
    angles = places.astype(jnp.float32)[:, None] * frequency[None, :]
    cosine = jnp.expand_dims(jnp.cos(angles), tuple(range(1, inputs.ndim - 1)))
    sine_part = jnp.expand_dims(jnp.sin(angles), tuple(range(1, inputs.ndim - 1)))
    widened = inputs.astype(jnp.float32)
    first_half = widened[..., :half_width]
    second_half = widened[..., half_width:]
    turned = jnp.concatenate([first_half * cosine - second_half * sine_part, second_half * cosine + first_half * sine_part], axis=-1)
    return turned.astype(jnp.bfloat16)


def document_ids(cu_seqlens, all_tokens):
    offsets = jnp.arange(all_tokens, dtype=jnp.int32)
    counted = jnp.sum((cu_seqlens[None, :] <= offsets[:, None]).astype(jnp.int32), axis=1)
    return (counted - 1).astype(jnp.int32)


def reference(queries, keys, values, cu_seqlens, positions):
    all_tokens = queries.shape[0]
    head_width = queries.shape[2]
    logit_scale = head_width ** -0.5
    owners = document_ids(cu_seqlens, all_tokens)
    rows = all_tokens // query_blocks
    reach = all_tokens // 8

    def one_head(triple):
        head_q, head_k, head_v = triple
        rotated_queries = lax.optimization_barrier(rotate(head_q, positions)).astype(jnp.float32)
        rotated_keys = lax.optimization_barrier(rotate(head_k, positions)).astype(jnp.float32)
        widened_values = head_v.astype(jnp.float32)
        pieces = []
        for block in range(query_blocks):
            first = block * rows
            stop = first + rows
            lowest = max(0, first - reach + 1)
            query_at = jnp.arange(first, stop, dtype=jnp.int32)
            key_at = jnp.arange(lowest, stop, dtype=jnp.int32)
            allowed = (query_at[:, None] >= key_at[None, :]) & (owners[first:stop, None] == owners[None, lowest:stop])
            attention_logits = jnp.dot(rotated_queries[first:stop], rotated_keys[lowest:stop].T) * logit_scale
            row_top = jnp.max(jnp.where(allowed, attention_logits, -1e30), axis=-1, keepdims=True)
            weights = jnp.where(allowed, jnp.exp(attention_logits - row_top), 0.0)
            softmax_denominator = jnp.sum(weights, axis=-1, keepdims=True)
            rounded_output = lax.optimization_barrier(weights.astype(jnp.bfloat16)).astype(jnp.float32)
            attention_result = jnp.dot(rounded_output, widened_values[lowest:stop]) / softmax_denominator
            pieces.append(attention_result.astype(jnp.bfloat16))
        return jnp.concatenate(pieces, axis=0)

    outputs = lax.map(one_head, (jnp.moveaxis(queries, 1, 0), jnp.moveaxis(keys, 1, 0), jnp.moveaxis(values, 1, 0)))
    return jnp.moveaxis(outputs, 0, 1)
```

```python
import functools

import jax
import jax.numpy as jnp
import numpy as np
from jax import lax
from jax.experimental import pallas as pl
from jax.experimental.pallas import tpu as pltpu
from jax.sharding import PartitionSpec as P

rope_base = 500000.0
head_pieces = 2
masked = -1e30

ANY = pl.BlockSpec(memory_space=pl.ANY)
VMEM = pl.BlockSpec(memory_space=pltpu.VMEM)
SMEM = pl.BlockSpec(memory_space=pltpu.SMEM)


def turn_tables(positions, width):
    half = width // 2
    ladder = jnp.arange(half, dtype=jnp.float32) * (2.0 / width)
    frequency = jnp.power(jnp.float32(rope_base), -ladder)
    angles = positions.astype(jnp.float32)[:, None] * frequency[None, :]
    cosine, sine = jnp.cos(angles), jnp.sin(angles)
    return jnp.concatenate([cosine, cosine], axis=1), jnp.concatenate([-sine, sine], axis=1)


def spread_kernel(turned, group, pieces, member, cosine, sine, *refs):
    inputs = refs[: len(turned)]
    rows = refs[-1]
    outs = refs[len(turned) : -1]
    tokens, _, width = inputs[0].shape
    heads = rows.shape[0] // tokens
    me = member[0]
    at = 0
    for peer in range(group):
        first = pl.multiple_of((me ^ peer) * heads, heads)
        parts = pieces[peer]
        for source in range(len(turned)):
            rows[...] = inputs[source][:, pl.ds(first, heads), :].astype(jnp.float32).reshape(tokens * heads, width)
            for head in range(heads):
                taken = rows[pl.ds(head, tokens, stride=heads), :]
                if turned[source]:
                    taken = taken * cosine[...] + pltpu.roll(taken, width // 2, 1) * sine[...]
                count = heads // parts
                out = outs[at + head // count]
                place = (source, head % count) if len(turned) > 1 else (head % count,)
                out[place] = taken.astype(jnp.bfloat16)
        at += parts


def spread(arrays, turned, group, pieces, member, cosine, sine):
    tokens, all_heads, width = arrays[0].shape
    heads = all_heads // group
    lead = (len(arrays),) if len(arrays) > 1 else ()
    shapes = []
    for peer in range(group):
        for _ in range(pieces[peer]):
            shapes.append(jax.ShapeDtypeStruct(lead + (heads // pieces[peer], tokens, width), jnp.bfloat16))
    outs = pl.pallas_call(
        functools.partial(spread_kernel, turned, group, pieces),
        out_shape=shapes,
        in_specs=[SMEM, VMEM, VMEM] + [VMEM] * len(arrays),
        out_specs=[VMEM] * len(shapes),
        scratch_shapes=[pltpu.VMEM((tokens * heads, width), jnp.float32)],
        name="spread",
    )(member, cosine, sine, *arrays)
    split, at = [], 0
    for peer in range(group):
        split.append(outs[at : at + pieces[peer]])
        at += pieces[peer]
    return split


def attend_kernel(group, heads, offsets, member, cu, *refs):
    early, own, asked = refs[:group], refs[group : 2 * group], refs[2 * group : 3 * group]
    outs = refs[3 * group : 4 * group]
    held, wanted, bias, result, head_sem, asked_sem, out_sem = refs[4 * group :]
    tokens, width = asked[0].shape[-2:]
    span = (group + 1) * tokens
    me = member[0]
    seat = me % group
    base = (me // group - 1) * (group * tokens)
    spots = cu.shape[0]

    for peer in range(group):
        pltpu.make_async_copy(
            asked[peer].at[pl.ds(offsets[2], heads)], wanted.at[seat ^ peer], asked_sem.at[peer]
        ).start()
    for head in range(heads):
        for peer in range(group):
            for side, (source, offset) in enumerate(((early[peer], offsets[0][peer]), (own[peer], offsets[1][peer]))):
                slot = pl.multiple_of((side * group + (seat ^ peer)) * tokens, tokens)
                pltpu.make_async_copy(
                    source.at[:, offset + head], held.at[:, head, pl.ds(slot, tokens), :], head_sem.at[head]
                ).start()

    def start_of(token):
        def later(at, best):
            return jnp.where(cu[at] <= token, cu[at], best)

        return lax.fori_loop(1, spots, later, cu[0])

    needed = []
    for block in range(group):
        first = base + (group + block) * tokens
        token = first + lax.broadcasted_iota(jnp.int32, (tokens, tokens), 0)
        begin = jnp.zeros((tokens, tokens), jnp.int32) + cu[0]
        for spot in range(1, spots):
            begin = jnp.where(token >= cu[spot], cu[spot], begin)
        for part in range(group + 1):
            at = base + (block + part) * tokens + lax.broadcasted_iota(jnp.int32, (tokens, tokens), 1)
            bias[block, :, part * tokens : (part + 1) * tokens] = jnp.where((at >= begin) & (at <= token), 0.0, masked)
        needed.append((first - start_of(first) + tokens - 1) // tokens + 1)

    sizes = sorted({min(2, group + 1), min(3, group + 1), group + 1})
    rate = np.float32(width**-0.5 * np.log2(np.e))

    for peer in range(group):
        pltpu.make_async_copy(
            asked[peer].at[pl.ds(offsets[2], heads)], wanted.at[seat ^ peer], asked_sem.at[peer]
        ).wait()

    def one_head(head, carry):
        pltpu.make_async_copy(held.at[:, head], held.at[:, head], head_sem.at[head]).wait()
        for block in range(group):

            def window(size, block=block):
                low = (group + 1 - size) * tokens
                keys = held[0, head, block * tokens + low : block * tokens + span, :]
                values = held[1, head, block * tokens + low : block * tokens + span, :]
                scores = lax.dot_general(
                    wanted[block, head], keys, (((1,), (1,)), ((), ())), preferred_element_type=jnp.float32
                )
                scores = scores + bias[block, :, low:]
                peak = jnp.max(scores, axis=1, keepdims=True)
                weights = jnp.exp2((scores - peak) * rate)
                total = jnp.sum(weights, axis=1, keepdims=True)
                mixed = jnp.dot(weights.astype(jnp.bfloat16), values, preferred_element_type=jnp.float32)
                result[block, head] = (mixed / total).astype(jnp.bfloat16)

            for at, size in enumerate(sizes):
                fits = needed[block] <= size
                if at > 0:
                    fits = fits & (needed[block] > sizes[at - 1])
                pl.when(fits)(functools.partial(window, size))
        return carry

    lax.fori_loop(0, heads, one_head, 0)
    for peer in range(group):
        pltpu.make_async_copy(result.at[seat ^ peer], outs[peer], out_sem.at[peer]).start()
    for peer in range(group):
        pltpu.make_async_copy(result.at[seat ^ peer], outs[peer], out_sem.at[peer]).wait()


def attend(group, heads, offsets, member, cu, early, own, asked):
    tokens, width = asked[0].shape[-2:]
    return pl.pallas_call(
        functools.partial(attend_kernel, group, heads, offsets),
        out_shape=[jax.ShapeDtypeStruct((heads, tokens, width), jnp.bfloat16)] * group,
        in_specs=[SMEM, SMEM] + [ANY] * (3 * group),
        out_specs=[ANY] * group,
        scratch_shapes=[
            pltpu.VMEM((2, heads, 2 * group * tokens, width), jnp.bfloat16),
            pltpu.VMEM((group, heads, tokens, width), jnp.bfloat16),
            pltpu.VMEM((group, tokens, (group + 1) * tokens), jnp.float32),
            pltpu.VMEM((group, heads, tokens, width), jnp.bfloat16),
            pltpu.SemaphoreType.DMA((heads,)),
            pltpu.SemaphoreType.DMA((group,)),
            pltpu.SemaphoreType.DMA((group,)),
        ],
        name="attend",
    )(member, cu, *early, *own, *asked)


def gather_kernel(group, runs, member, *refs):
    rows, out = refs[-1], refs[-2]
    tokens, _, width = out.shape
    heads = rows.shape[0] // tokens
    count = heads // runs
    me = member[0]
    for peer in range(group):
        for head in range(heads):
            piece = refs[peer * runs + head // count]
            rows[pl.ds(head, tokens, stride=heads), :] = piece[head % count].astype(jnp.float32)
        first = pl.multiple_of((me ^ peer) * heads, heads)
        out[:, pl.ds(first, heads), :] = rows[...].reshape(tokens, heads, width).astype(jnp.bfloat16)


def gather(pieces, group, runs, member, shape):
    tokens, all_heads, width = shape
    return pl.pallas_call(
        functools.partial(gather_kernel, group, runs),
        out_shape=jax.ShapeDtypeStruct(shape, jnp.bfloat16),
        in_specs=[SMEM] + [VMEM] * len(pieces),
        out_specs=VMEM,
        scratch_shapes=[pltpu.VMEM((tokens * all_heads // group, width), jnp.float32)],
        name="gather",
    )(member, *pieces)


def on_device(queries, keys, values, cu_seqlens, positions):
    devices = lax.axis_size("ctx")
    tokens, all_heads, width = queries.shape
    reach = tokens * devices // 8
    group = reach // tokens
    heads = all_heads // group
    count = heads // head_pieces
    me = lax.axis_index("ctx").astype(jnp.int32)
    seat = (me % group)[None]
    me = me[None]
    swap = [[(device, device ^ peer) for device in range(devices)] for peer in range(group)]
    onward = [(device, device + group) for device in range(devices - group)]

    def send(array, pairs):
        return lax.ppermute(array, "ctx", pairs)

    pieces = tuple(1 if peer < 2 else head_pieces for peer in range(group))
    cosine, sine = turn_tables(positions, width)
    stored = spread((keys, values), (True, False), group, pieces, seat, cosine, sine)
    asked = spread((queries,), (True,), group, (1,) * group, seat, cosine, sine)

    own = [list(stored[peer]) for peer in range(group)]
    early = [[] for _ in range(group)]
    for peer in range(group):
        for piece in range(pieces[peer]):
            if peer > 0:
                own[peer][piece] = send(stored[peer][piece], swap[peer])
            early[peer].append(send(own[peer][piece], onward))
    asked = [asked[0][0]] + [send(asked[peer][0], swap[peer]) for peer in range(1, group)]

    back = [[] for _ in range(group)]
    for piece in range(head_pieces):
        starts = tuple(piece * count if pieces[peer] == 1 else 0 for peer in range(group))
        picked = [own[peer][0 if pieces[peer] == 1 else piece] for peer in range(group)]
        before = [early[peer][0 if pieces[peer] == 1 else piece] for peer in range(group)]
        mixed = attend(group, count, (starts, starts, piece * count), me, cu_seqlens, before, picked, asked)
        for peer in range(group):
            back[peer].append(mixed[peer] if peer == 0 else send(mixed[peer], swap[peer]))
    flat = [array for peer in range(group) for array in back[peer]]
    return gather(flat, group, head_pieces, seat, queries.shape)


def solution(mesh):
    return jax.shard_map(
        on_device,
        mesh=mesh,
        in_specs=(P("ctx", None, None), P("ctx", None, None), P("ctx", None, None), P(), P("ctx")),
        out_specs=P("ctx", None, None),
        check_vma=False,
    )
```

```python
import functools

import jax
import jax.numpy as jnp
import numpy as np
from jax import lax
from jax.experimental import pallas as pl
from jax.experimental.pallas import tpu as pltpu
from jax.sharding import PartitionSpec as P

rope_base = 500000.0
head_pieces = 2
masked = -1e30
near_most = 2**21

ANY = pl.BlockSpec(memory_space=pl.ANY)
VMEM = pl.BlockSpec(memory_space=pltpu.VMEM)
SMEM = pl.BlockSpec(memory_space=pltpu.SMEM)


def turn_tables(positions, width):
    half = width // 2
    lane = jnp.arange(width, dtype=jnp.int32)
    ladder = (lane % half).astype(jnp.float32) * (2.0 / width)
    frequency = jnp.power(jnp.float32(rope_base), -ladder)
    angles = positions.astype(jnp.float32)[:, None] * frequency[None, :]
    return jnp.cos(angles), jnp.where(lane[None, :] < half, -jnp.sin(angles), jnp.sin(angles))


def shape_of(near, shape, dtype=jnp.bfloat16):
    return pltpu.VMEM(shape, dtype) if near else jax.ShapeDtypeStruct(shape, dtype)


def held_near(near, arrays):
    return [pltpu.with_memory_space_constraint(array, pltpu.VMEM) for array in arrays] if near else list(arrays)


def room(near):
    return pltpu.CompilerParams(vmem_limit_bytes=20 * 2**20) if near else None


def spread_kernel(turned, peers, pieces, cosine, sine, *refs):
    many = len(turned)
    inputs, outs, (taken, rows, sem) = refs[:many], refs[many:-3], refs[-3:]
    tokens, _, width = inputs[0].shape
    heads = taken.shape[-2]
    group = inputs[0].shape[1] // heads
    seat = lax.axis_index("ctx") % group
    copies = {}
    for at, peer in enumerate(peers):
        first = pl.multiple_of((seat ^ peer) * heads, heads)
        for source in range(many):
            copies[at, source] = pltpu.make_async_copy(
                inputs[source].at[:, pl.ds(first, heads), :], taken.at[at, source], sem.at[at, source]
            )
            copies[at, source].start()
    out_at = 0
    for at, peer in enumerate(peers):
        count = heads // pieces[peer]
        for source in range(many):
            copies[at, source].wait()
            slot = (at * many + source) % rows.shape[0]
            rows[slot] = taken[at, source].astype(jnp.float32).reshape(tokens * heads, width)
            for head in range(heads):
                values = rows[slot, pl.ds(head, tokens, stride=heads), :]
                if turned[source]:
                    values = values * cosine[...] + pltpu.roll(values, width // 2, 1) * sine[...]
                place = (source, head % count) if many > 1 else (head % count,)
                outs[out_at + head // count][place] = values.astype(jnp.bfloat16)
        out_at += pieces[peer]


def spread(near, arrays, turned, peers, pieces, group, cosine, sine):
    tokens, all_heads, width = arrays[0].shape
    heads = all_heads // group
    many = len(arrays)
    lead = (many,) if many > 1 else ()
    shapes = [
        shape_of(near, lead + (heads // pieces[peer], tokens, width)) for peer in peers for _ in range(pieces[peer])
    ]
    outs = pl.pallas_call(
        functools.partial(spread_kernel, turned, peers, pieces),
        out_shape=shapes,
        in_specs=[VMEM, VMEM] + [ANY] * many,
        out_specs=[VMEM] * len(shapes),
        scratch_shapes=[
            pltpu.VMEM((len(peers), many, tokens, heads, width), jnp.bfloat16),
            pltpu.VMEM((min(4, many * len(peers)), tokens * heads, width), jnp.float32),
            pltpu.SemaphoreType.DMA((len(peers), many)),
        ],
        compiler_params=room(near),
        name="spread",
    )(cosine, sine, *arrays)
    split, at = {}, 0
    for peer in peers:
        split[peer] = list(outs[at : at + pieces[peer]])
        at += pieces[peer]
    return split


def mask_kernel(group, cu, bias, needed):
    tokens = bias.shape[1]
    me = lax.axis_index("ctx")
    base = (me // group - 1) * (group * tokens)
    spots = cu.shape[0]
    for block in range(group):
        first = base + (group + block) * tokens
        token = first + lax.broadcasted_iota(jnp.int32, (tokens, tokens), 0)
        begin = jnp.zeros((tokens, tokens), jnp.int32) + cu[0]
        start = cu[0]
        for spot in range(1, spots):
            begin = jnp.where(token >= cu[spot], cu[spot], begin)
            start = jnp.where(first >= cu[spot], cu[spot], start)
        for part in range(group + 1):
            at = base + (block + part) * tokens + lax.broadcasted_iota(jnp.int32, (tokens, tokens), 1)
            bias[block, :, part * tokens : (part + 1) * tokens] = jnp.where((at >= begin) & (at <= token), 0.0, masked)
        needed[block] = (first - start + tokens - 1) // tokens + 1


def mask(near, group, tokens, cu):
    return pl.pallas_call(
        functools.partial(mask_kernel, group),
        out_shape=[
            shape_of(near, (group, tokens, (group + 1) * tokens), jnp.float32),
            jax.ShapeDtypeStruct((group,), jnp.int32),
        ],
        in_specs=[SMEM],
        out_specs=[VMEM, SMEM],
        compiler_params=room(near),
        name="mask",
    )(cu)


def attend_kernel(group, heads, offsets, needed, *refs):
    early, own, asked = refs[:group], refs[group : 2 * group], refs[2 * group : 3 * group]
    bias = refs[3 * group]
    outs = refs[3 * group + 1 : 4 * group + 1]
    held, wanted, result, key_sem, asked_sem, out_sem = refs[4 * group + 1 :]
    tokens, width = asked[0].shape[-2:]
    seat = lax.axis_index("ctx") % group

    copies = []
    for peer in range(group):
        for side, (source, offset) in enumerate(((early[peer], offsets[0][peer]), (own[peer], offsets[1][peer]))):
            slot = pl.multiple_of((side * group + (seat ^ peer)) * tokens, tokens)
            copies.append(
                pltpu.make_async_copy(
                    source.at[:, pl.ds(offset, heads)], held.at[:, :, pl.ds(slot, tokens), :], key_sem.at[side, peer]
                )
            )
        copies.append(
            pltpu.make_async_copy(
                asked[peer].at[pl.ds(offsets[2], heads)], wanted.at[seat ^ peer], asked_sem.at[peer]
            )
        )
    for copy in copies:
        copy.start()
    for copy in copies:
        copy.wait()

    sizes = sorted({min(2, group + 1), min(3, group + 1), group + 1})
    rate = np.float32(width**-0.5 * np.log2(np.e))

    def one_block(block, carry):
        def window(size):
            low = (group + 1 - size) * tokens
            at = pl.multiple_of(block * tokens + low, tokens)
            keep = pl.ds(at, size * tokens)
            allowed = bias[block, :, low:]
            scores = [
                lax.dot_general(
                    wanted[block, head], held[0, head, keep, :], (((1,), (1,)), ((), ())), preferred_element_type=jnp.float32
                )
                + allowed
                for head in range(heads)
            ]
            peaks = [jnp.max(one, axis=1, keepdims=True) for one in scores]
            weights = [jnp.exp2((one - peak) * rate) for one, peak in zip(scores, peaks)]
            totals = [jnp.sum(one, axis=1, keepdims=True) for one in weights]
            for head in range(heads):
                mixed = jnp.dot(
                    weights[head].astype(jnp.bfloat16), held[1, head, keep, :], preferred_element_type=jnp.float32
                )
                result[block, head] = (mixed / totals[head]).astype(jnp.bfloat16)

        for at, size in enumerate(sizes):
            fits = needed[block] <= size
            if at > 0:
                fits = fits & (needed[block] > sizes[at - 1])
            pl.when(fits)(functools.partial(window, size))
        mine = [pltpu.make_async_copy(result.at[block], outs[peer], out_sem.at[peer]) for peer in range(group)]
        for peer in range(group):
            pl.when(block == seat ^ peer)(mine[peer].start)
        return carry

    lax.fori_loop(0, group, one_block, 0)
    for peer in range(group):
        pltpu.make_async_copy(result.at[seat ^ peer], outs[peer], out_sem.at[peer]).wait()


def attend(near, group, heads, offsets, needed, bias, early, own, asked):
    tokens, width = asked[0].shape[-2:]
    return pl.pallas_call(
        functools.partial(attend_kernel, group, heads, offsets),
        out_shape=[shape_of(near, (heads, tokens, width))] * group,
        in_specs=[SMEM] + [VMEM if near else ANY] * (3 * group) + [VMEM],
        out_specs=[VMEM if near else ANY] * group,
        scratch_shapes=[
            pltpu.VMEM((2, heads, 2 * group * tokens, width), jnp.bfloat16),
            pltpu.VMEM((group, heads, tokens, width), jnp.bfloat16),
            pltpu.VMEM((group, heads, tokens, width), jnp.bfloat16),
            pltpu.SemaphoreType.DMA((2, group)),
            pltpu.SemaphoreType.DMA((group,)),
            pltpu.SemaphoreType.DMA((group,)),
        ],
        compiler_params=room(near),
        name="attend",
    )(needed, *held_near(near, [*early, *own, *asked, bias]))


def gather_kernel(group, runs, *refs):
    rows, out = refs[-1], refs[-2]
    tokens, _, width = out.shape
    heads = rows.shape[1] // tokens
    seat = lax.axis_index("ctx") % group
    for peer in range(group):
        slot = peer % rows.shape[0]
        head = 0
        for piece in refs[peer * runs : (peer + 1) * runs]:
            for one in range(piece.shape[0]):
                rows[slot, pl.ds(head, tokens, stride=heads), :] = piece[one].astype(jnp.float32)
                head += 1
        first = pl.multiple_of((seat ^ peer) * heads, heads)
        out[:, pl.ds(first, heads), :] = rows[slot].reshape(tokens, heads, width).astype(jnp.bfloat16)


def gather(near, pieces, group, runs, shape):
    tokens, all_heads, width = shape
    return pl.pallas_call(
        functools.partial(gather_kernel, group, runs),
        out_shape=jax.ShapeDtypeStruct(shape, jnp.bfloat16),
        in_specs=[VMEM] * len(pieces),
        out_specs=VMEM,
        scratch_shapes=[pltpu.VMEM((min(4, group), tokens * all_heads // group, width), jnp.float32)],
        compiler_params=room(near),
        name="gather",
    )(*held_near(near, pieces))


def on_device(queries, keys, values, cu_seqlens, positions):
    devices = lax.axis_size("ctx")
    tokens, all_heads, width = queries.shape
    reach = tokens * devices // 8
    group = reach // tokens
    heads = all_heads // group
    count = heads // head_pieces
    near = 2 * queries.size <= near_most
    swap = [[(device, device ^ peer) for device in range(devices)] for peer in range(group)]
    onward = [(device, device + group) for device in range(devices - group)]

    def send(array, pairs):
        return lax.ppermute(array, "ctx", pairs)

    pieces = tuple(1 if peer < 2 else head_pieces for peer in range(group))
    cosine, sine = turn_tables(positions, width)
    both, turned = (keys, values), (True, False)
    stored = spread(near, both, turned, (0,), pieces, group, cosine, sine)
    own, early = {0: stored[0]}, {0: [send(stored[0][0], onward)]}
    stored = spread(near, both, turned, tuple(range(1, group)), pieces, group, cosine, sine)
    for peer in range(1, group):
        own[peer] = [send(array, swap[peer]) for array in stored[peer]]
        early[peer] = [send(array, onward) for array in own[peer]]
    asked = spread(near, (queries,), (True,), tuple(range(group)), (1,) * group, group, cosine, sine)
    asked = [asked[0][0]] + [send(asked[peer][0], swap[peer]) for peer in range(1, group)]
    bias, needed = mask(near, group, tokens, cu_seqlens)

    back = [[] for _ in range(group)]
    for piece in range(head_pieces):
        starts = tuple(piece * count if pieces[peer] == 1 else 0 for peer in range(group))
        picked = [own[peer][0 if pieces[peer] == 1 else piece] for peer in range(group)]
        before = [early[peer][0 if pieces[peer] == 1 else piece] for peer in range(group)]
        mixed = attend(near, group, count, (starts, starts, piece * count), needed, bias, before, picked, asked)
        for peer in range(group):
            back[peer].append(mixed[peer] if peer == 0 else send(mixed[peer], swap[peer]))
    flat = [array for peer in range(group) for array in back[peer]]
    return gather(near, flat, group, head_pieces, queries.shape)


def solution(mesh):
    return jax.shard_map(
        on_device,
        mesh=mesh,
        in_specs=(P("ctx", None, None), P("ctx", None, None), P("ctx", None, None), P(), P("ctx")),
        out_specs=P("ctx", None, None),
        check_vma=False,
    )
```
